512 devices in a mesh: mode: 8 (over x, core), ax: 32 (over y, z_hi), rad: 2 (over z_lo).
Axes of the slice: x: 4, y: 8, z: 8 (z_hi: 4, z_lo: 2; z = z_hi * 2 + z_lo), core: 2. Of those that a mesh axis runs over, the one named last changes fastest.
Arguments:
- adjoint: float32 [5, 256, 128, 256], P(None, 'mode', 'ax', 'rad'), may hold values from -6 to 6
- state: float32 [5, 256, 128, 256], P(None, 'mode', 'ax', 'rad'), may hold values from -6 to 6
- wake: float32 [256, 128, 256], P('mode', 'ax', 'rad'), may hold values from 0.2 to 1.5
- jac_axial: float32 [5, 5], replicated, may hold values from -2.5 to 2.5
- jac_radial: float32 [5, 5], replicated, may hold values from -2.5 to 2.5
- jac_swirl: float32 [5, 5], replicated, may hold values from -2.5 to 2.5
- wake_coupling: float32 [5, 5], replicated, may hold values from -2.5 to 2.5
Outputs:
- adjoint_in: float32 [5, 256, 128, 256], P(None, 'mode', 'ax', 'rad')
- wake_grad: float32 [256, 128, 256], P('mode', 'ax', 'rad')
The draws below stay inside these ranges and needn't reach their ends.
All inputs are finite; a program needn't handle non-finite values.
Results may differ from the reference program's by a relative error of at most 0.000098.
Values sent between devices are 32-bit elements; how exact they have to be, the bound alone decides.
A program may use at most 64 MiB of HBM per device.

```python
import math
import jax
import jax.numpy as jnp
from jax import lax

F = 5
M = 256
CXD = 4
NX = 128
NR = 256


def levels(rng, dims, shards, smallest, largest):
    level, own = 1.0, jax.random.fold_in(rng, 6)
    for position, shards_of in shards:
        steps = jnp.exp(jax.random.uniform(jax.random.fold_in(own, position), (shards_of,), jnp.float32, smallest / len(shards), largest / len(shards)))
        level = level * jnp.repeat(steps, dims[position] // shards_of).reshape([-1 if axis == position else 1 for axis in range(len(dims))])
    return level


def normal_values(stream_key, extent, width, bound, pieces=(), kind=jnp.bfloat16):
    entries = width * jax.random.normal(stream_key, extent, jnp.float32)
    if pieces:
        entries = entries * levels(stream_key, extent, pieces, -0.22, 0.18)
    return jnp.clip(entries, -bound, bound).astype(kind)


def setup_inputs(seed: int = 0) -> dict:
    keys = jax.random.split(jax.random.key(seed), 8)
    adjoint = normal_values(keys[0], (F, M, NX, NR), 1.0, 6.0, ((1, 8), (2, 32), (3, 2)), jnp.float32)
    state = normal_values(keys[1], (F, M, NX, NR), 1.0, 6.0, ((1, 8), (2, 32), (3, 2)), jnp.float32)
    wake = jnp.clip(0.2 + 1.3 * jax.random.uniform(keys[2], (M, NX, NR), jnp.float32) ** levels(keys[2], (M, NX, NR), ((0, 8), (1, 32), (2, 2)), -0.2, 0.2), 0.2, 1.5)
    jac_axial = normal_values(keys[3], (F, F), F ** -0.5, 2.5, (), jnp.float32)
    jac_radial = normal_values(keys[4], (F, F), F ** -0.5, 2.5, (), jnp.float32)
    jac_swirl = normal_values(keys[5], (F, F), F ** -0.5, 2.5, (), jnp.float32)
    wake_coupling = normal_values(keys[6], (F, F), F ** -0.5, 2.5, (), jnp.float32)
    return dict(adjoint=adjoint, state=state, wake=wake, jac_axial=jac_axial, jac_radial=jac_radial, jac_swirl=jac_swirl, wake_coupling=wake_coupling)


exact_prec = lax.Precision.HIGHEST

def fourier_basis(mode_count):
    angle_idx = jnp.arange(mode_count, dtype=jnp.int32)[:, None]
    coef_idx = jnp.arange(mode_count, dtype=jnp.int32)[None, :]
    orders = coef_idx // 2
    phases = (orders * angle_idx % mode_count).astype(jnp.float32) * jnp.float32(2.0 * math.pi / mode_count)
    scale_two = jnp.float32(math.sqrt(2.0 / mode_count))
    scale_one = jnp.float32(1.0 / math.sqrt(mode_count))
    table = jnp.where(coef_idx % 2 == 0, scale_two * jnp.cos(phases), scale_two * jnp.sin(phases))
    table = jnp.where(coef_idx == 0, scale_one, table)
    signs = jnp.where(angle_idx % 2 == 0, scale_one, -scale_one)
    table = jnp.where(coef_idx == 1, signs, table)
    return table

def rotate(field, first_order, mode_count):
    fields, modes_here, cells_ax, cells_rad = field.shape
    paired = field.reshape(fields, modes_here // 2, 2, cells_ax, cells_rad)
    orders = (first_order + jnp.arange(modes_here // 2, dtype=jnp.int32)).astype(jnp.float32) / jnp.float32(mode_count // 2)
    orders = orders[None, :, None, None]
    turned = jnp.stack([orders * paired[:, :, 1], -orders * paired[:, :, 0]], axis=2)
    return turned.reshape(fields, modes_here, cells_ax, cells_rad)

def reference(adjoint, state, wake, jac_axial, jac_radial, jac_swirl, wake_coupling):
    padded = jnp.pad(adjoint, ((0, 0), (0, 0), (1, 1), (1, 1)))
    axial_diff = 0.5 * (padded[:, :, 2:, 1:-1] - padded[:, :, :-2, 1:-1])
    radial_diff = 0.5 * (padded[:, :, 1:-1, 2:] - padded[:, :, 1:-1, :-2])
    radius = 0.5 + (jnp.arange(NR, dtype=jnp.int32).astype(jnp.float32) + 0.5) / jnp.float32(2.0 * NR)
    swirl_rate = 0.25 / radius
    turned = rotate(adjoint, 0, M) * swirl_rate
    transport = jnp.einsum('ef,ekxr->fkxr', jac_axial, axial_diff, precision=exact_prec)
    transport = transport + jnp.einsum('ef,ekxr->fkxr', jac_radial, radial_diff, precision=exact_prec)
    transport = transport + jnp.einsum('ef,ekxr->fkxr', jac_swirl, turned, precision=exact_prec)
    coupled = jnp.einsum('fe,ekxr->fkxr', wake_coupling, state, precision=exact_prec)
    basis_table = fourier_basis(M)

    def block_part(offset):
        adj_part = lax.dynamic_slice_in_dim(adjoint, offset, CXD, 2)
        cpl_part = lax.dynamic_slice_in_dim(coupled, offset, CXD, 2)
        wake_part = lax.dynamic_slice_in_dim(wake, offset, CXD, 1)
        adj_angle = jnp.einsum('tk,fkxr->ftxr', basis_table, adj_part, precision=exact_prec)
        cpl_angle = jnp.einsum('tk,fkxr->ftxr', basis_table, cpl_part, precision=exact_prec)
        returned = jnp.einsum('tk,ftxr->fkxr', basis_table, wake_part[None] * adj_angle, precision=exact_prec)
        grad_part = -lax.optimization_barrier(jnp.sum(adj_angle * cpl_angle, axis=0))
        return (returned, grad_part)
    offsets = jnp.arange(NX // CXD, dtype=jnp.int32) * CXD
    returned_all, grad_all = lax.map(block_part, offsets)
    returned = jnp.moveaxis(returned_all, 0, 2).reshape(F, M, NX, NR)
    wake_grad = jnp.moveaxis(grad_all, 0, 1).reshape(M, NX, NR)
    adjoint_in = adjoint + transport - jnp.einsum('ef,ekxr->fkxr', wake_coupling, returned, precision=exact_prec)
    return (adjoint_in, wake_grad)
```

```python
import functools
import math

import jax
import jax.numpy as jnp
import ml_dtypes
import numpy as np
from jax import lax
from jax.experimental import pallas as pl
from jax.experimental.pallas import tpu as pltpu
from jax.sharding import PartitionSpec as P

MESH = pl.DeviceIdType.MESH
F, K, X, L = 5, 32, 4, 128
D = 8
HALF = L // 2
PAIRS = 3
ORDER = (4, 5, 3, 2, 6, 7, 1)


def basis_parts():
    t = np.arange(D * K)[:, None]
    k = np.arange(D * K)[None, :]
    phase = ((k // 2) * t % (D * K)) * (2.0 * math.pi / (D * K))
    table = math.sqrt(2.0 / (D * K)) * np.where(k % 2 == 0, np.cos(phase), np.sin(phase))
    one = 1.0 / math.sqrt(D * K)
    table = np.where(k == 0, one, table)
    table = np.where(k == 1, np.where(t % 2 == 0, one, -one), table)
    high = table.astype(ml_dtypes.bfloat16)
    low = (table - high.astype(np.float64)).astype(ml_dtypes.bfloat16)
    return high, low


def product(high, low, x):
    x_high = x.astype(jnp.bfloat16)
    x_low = (x - x_high.astype(jnp.float32)).astype(jnp.bfloat16)
    dot = functools.partial(jnp.dot, preferred_element_type=jnp.float32)
    return dot(high, x_high) + (dot(high, x_low) + dot(low, x_high))


def kernel(
    adj_ref, state_ref, wake_ref, bh_ref, bl_ref, th_ref, tl_ref, ja_ref, jr_ref, js_ref, wc_ref,
    out_ref, grad_ref,
    send, recv, wsend, wrecv, wfull, back, ret, hsend, hrecv, esend, erecv, acc,
    f_ssem, f_rsem, w_ssem, w_rsem, b_ssem, b_rsem, h_ssem, h_rsem, e_ssem, e_rsem,
):
    me = lax.axis_index("mode")
    ax = lax.axis_index("ax")
    rad = lax.axis_index("rad")
    ax_count = lax.axis_size("ax")
    ax_up = lax.rem(ax + 1, ax_count)
    ax_down = lax.rem(ax + ax_count - 1, ax_count)
    others = [lax.rem(me + i, D) for i in ORDER]

    barrier = pltpu.get_barrier_semaphore()
    for other in others:
        pl.semaphore_signal(barrier, inc=1, device_id={"mode": other}, device_id_type=MESH)
    pl.semaphore_signal(barrier, inc=1, device_id={"ax": ax_up}, device_id_type=MESH)
    pl.semaphore_signal(barrier, inc=1, device_id={"ax": ax_down}, device_id_type=MESH)
    pl.semaphore_signal(barrier, inc=1, device_id={"rad": 1 - rad}, device_id_type=MESH)

    lane = lax.broadcasted_iota(jnp.int32, (K, L), 1)
    low_half = lane < HALF

    def cells(ref, f, x):
        return ref[f, pl.ds(x, K, stride=X), :]

    def swap(v):
        return pltpu.roll(v, HALF, axis=1)

    edge = jnp.zeros((K, L), jnp.float32)
    for f in range(F):
        hsend[0, f] = cells(adj_ref, f, 0)
        hsend[1, f] = cells(adj_ref, f, X - 1)
        for x in range(X):
            s = f * X + x
            v = cells(adj_ref, f, x)
            v = jnp.where(rad == 0, pltpu.roll(v, s + 1, axis=1), pltpu.roll(v, s, axis=1) if s else v)
            edge = jnp.where(lane == s, v, edge)
    esend[...] = edge

    q = K // 2
    for x in range(X):
        w = wake_ref[pl.ds(x, K, stride=X), :]
        w_swap = swap(w)
        m = low_half[:q]
        wsend[2 * x] = jnp.where(m, w[:q], w_swap[q:])
        wsend[2 * x + 1] = jnp.where(m, w_swap[:q], w[q:])
        states = [cells(state_ref, e, x) for e in range(F)]
        for f in range(F):
            a = cells(adj_ref, f, x)
            c = wc_ref[f, 0] * states[0]
            for e in range(1, F):
                c = c + wc_ref[f, e] * states[e]
            send[f, 2 * x] = jnp.where(low_half, a, swap(c))
            send[f, 2 * x + 1] = jnp.where(low_half, swap(a), c)

    pl.semaphore_wait(barrier, D + 2)

    started = []

    def go(src, dst, ssem, rsem, device):
        copy = pltpu.make_async_remote_copy(
            src_ref=src, dst_ref=dst, send_sem=ssem, recv_sem=rsem, device_id=device, device_id_type=MESH
        )
        copy.start()
        started.append(copy)

    go(hsend.at[0], hrecv.at[1], h_ssem.at[0], h_rsem.at[1], {"ax": ax_down})
    go(hsend.at[1], hrecv.at[0], h_ssem.at[1], h_rsem.at[0], {"ax": ax_up})
    go(esend, erecv, e_ssem, e_rsem, {"rad": 1 - rad})
    for other in others:
        go(wsend.at[other], wrecv.at[me], w_ssem.at[other], w_rsem.at[me], {"mode": other})
    for f in range(F):
        for other in others:
            go(send.at[f, other], recv.at[f, me], f_ssem.at[f, other], f_rsem.at[f, me], {"mode": other})

    wrecv[me] = wsend[me]
    for f in range(F):
        recv[f, me] = send[f, me]

    def arrived(ref, sem):
        pltpu.make_async_remote_copy(
            src_ref=ref, dst_ref=ref, send_sem=sem, recv_sem=sem, device_id={"mode": me}, device_id_type=MESH
        ).wait_recv()

    for other in others:
        arrived(wrecv.at[other], w_rsem.at[other])
    for d in range(D):
        w = wrecv[d]
        w_swap = swap(w)
        m = low_half[:q]
        wfull[pl.ds(d * K, q), :] = jnp.where(m, w, w_swap)
        wfull[pl.ds(d * K + q, q), :] = jnp.where(m, w_swap, w)

    low_all = lax.broadcasted_iota(jnp.int32, (D * K, L), 1) < HALF
    total = None
    first = None
    for f in range(F):
        for other in others:
            arrived(recv.at[f, other], f_rsem.at[f, other])
        angle = product(bh_ref[...], bl_ref[...], recv[f].reshape(D * K, L))
        angle_swap = swap(angle)
        term = angle * angle_swap
        total = term if total is None else total + term
        wake_all = wfull[...]
        if f % 2 == 0 and f < F - 1:
            first = wake_all * angle
            continue
        p = f // 2
        if f < F - 1:
            both = jnp.where(low_all, first, wake_all * angle_swap)
        else:
            both = wake_all * angle
        result = product(th_ref[...], tl_ref[...], both)
        if f == F - 1:
            result = jnp.where(low_all, result, -total)
        back[p] = result.reshape(D, K, L)
        for other in others:
            go(back.at[p, other], ret.at[p, me], b_ssem.at[p, other], b_rsem.at[p, me], {"mode": other})
        ret[p, me] = back[p, me]

    arrived(hrecv.at[0], h_rsem.at[0])
    arrived(hrecv.at[1], h_rsem.at[1])
    arrived(erecv, e_rsem)
    row = lax.broadcasted_iota(jnp.int32, (K, L), 0)
    even = lax.rem(row, 2) == 0
    order = lax.div(me * K + row, 2).astype(jnp.float32) / jnp.float32(D * K // 2)
    radius = 0.5 + ((rad * L + lane).astype(jnp.float32) + 0.5) / jnp.float32(4.0 * L)
    rate = (0.25 / radius) * order
    rate = jnp.where(even, rate, -rate)
    nearby = erecv[...]
    nearby_up = jnp.where(rad == 0, nearby, 0.0)
    nearby_down = jnp.where(rad == 1, nearby, 0.0)
    for x in range(X):
        fields, axial, radial, turned = [], [], [], []
        for e in range(F):
            a = cells(adj_ref, e, x)
            fields.append(a)
            if x == X - 1:
                above = jnp.where(ax < ax_count - 1, hrecv[1, e], 0.0)
            else:
                above = cells(adj_ref, e, x + 1)
            if x == 0:
                below = jnp.where(ax > 0, hrecv[0, e], 0.0)
            else:
                below = cells(adj_ref, e, x - 1)
            axial.append(0.5 * (above - below))
            s = e * X + x
            up = jnp.where(lane == L - 1, pltpu.roll(nearby_up, L - 1 - s, axis=1), pltpu.roll(a, L - 1, axis=1))
            edge_down = pltpu.roll(nearby_down, L - s, axis=1) if s else nearby_down
            down = jnp.where(lane == 0, edge_down, pltpu.roll(a, 1, axis=1))
            radial.append(0.5 * (up - down))
            turned.append(rate * jnp.where(even, pltpu.roll(a, K - 1, axis=0), pltpu.roll(a, 1, axis=0)))
        for f in range(F):
            v = fields[f]
            for e in range(F):
                v = v + ja_ref[e, f] * axial[e] + jr_ref[e, f] * radial[e] + js_ref[e, f] * turned[e]
            acc[f, x] = v

    for p in range(PAIRS):
        for other in others:
            arrived(ret.at[p, other], b_rsem.at[p, other])
    for x in range(X):
        returned = []
        for p in range(PAIRS):
            one, two = ret[p, 2 * x], ret[p, 2 * x + 1]
            returned.append(jnp.where(low_half, one, swap(two)))
            returned.append(jnp.where(low_half, swap(one), two))
        grad_ref[pl.ds(x, K, stride=X), :] = returned[F]
        for f in range(F):
            v = acc[f, x]
            for e in range(F):
                v = v - wc_ref[e, f] * returned[e]
            out_ref[f, pl.ds(x, K, stride=X), :] = v

    for copy in started:
        copy.wait_send()


def body(adjoint, state, wake, jac_axial, jac_radial, jac_swirl, wake_coupling):
    high, low = basis_parts()
    vmem = pl.BlockSpec(memory_space=pltpu.VMEM)
    smem = pl.BlockSpec(memory_space=pltpu.SMEM)
    dma = pltpu.SemaphoreType.DMA
    f32 = jnp.float32
    adjoint_in, grad = pl.pallas_call(
        kernel,
        out_shape=(
            jax.ShapeDtypeStruct((F, K * X, L), f32),
            jax.ShapeDtypeStruct((K * X, L), f32),
        ),
        in_specs=[vmem] * 7 + [smem] * 4,
        out_specs=(vmem, vmem),
        scratch_shapes=[
            pltpu.VMEM((F, D, K, L), f32),
            pltpu.VMEM((F, D, K, L), f32),
            pltpu.VMEM((D, K // 2, L), f32),
            pltpu.VMEM((D, K // 2, L), f32),
            pltpu.VMEM((D * K, L), f32),
            pltpu.VMEM((PAIRS, D, K, L), f32),
            pltpu.VMEM((PAIRS, D, K, L), f32),
            pltpu.VMEM((2, F, K, L), f32),
            pltpu.VMEM((2, F, K, L), f32),
            pltpu.VMEM((K, L), f32),
            pltpu.VMEM((K, L), f32),
            pltpu.VMEM((F, X, K, L), f32),
            dma((F, D)), dma((F, D)), dma((D,)), dma((D,)), dma((PAIRS, D)), dma((PAIRS, D)),
            dma((2,)), dma((2,)), dma, dma,
        ],
        compiler_params=pltpu.CompilerParams(
            collective_id=0, has_side_effects=True, vmem_limit_bytes=32 * 1024 * 1024
        ),
        name="section_adjoint",
    )(
        adjoint.reshape(F, K * X, L), state.reshape(F, K * X, L), wake.reshape(K * X, L),
        jnp.asarray(high), jnp.asarray(low), jnp.asarray(np.ascontiguousarray(high.T)),
        jnp.asarray(np.ascontiguousarray(low.T)), jac_axial, jac_radial, jac_swirl, wake_coupling,
    )
    return adjoint_in.reshape(adjoint.shape), grad.reshape(wake.shape)


def solution(mesh):
    return jax.shard_map(
        body,
        mesh=mesh,
        in_specs=(
            P(None, "mode", "ax", "rad"),
            P(None, "mode", "ax", "rad"),
            P("mode", "ax", "rad"),
            P(),
            P(),
            P(),
            P(),
        ),
        out_specs=(P(None, "mode", "ax", "rad"), P("mode", "ax", "rad")),
        check_vma=False,
    )
```

```python
import functools
import math

import jax
import jax.numpy as jnp
import ml_dtypes
import numpy as np
from jax import lax
from jax.experimental import pallas as pl
from jax.experimental.pallas import tpu as pltpu
from jax.sharding import PartitionSpec as P

MESH = pl.DeviceIdType.MESH
F, K, X, L = 5, 32, 4, 128
D = 8
HALF = L // 2
PAIRS = 3
ORDER = (4, 5, 3, 2, 6, 7, 1)


def basis_parts():
    t = np.arange(D * K)[:, None]
    k = np.arange(D * K)[None, :]
    phase = ((k // 2) * t % (D * K)) * (2.0 * math.pi / (D * K))
    table = math.sqrt(2.0 / (D * K)) * np.where(k % 2 == 0, np.cos(phase), np.sin(phase))
    one = 1.0 / math.sqrt(D * K)
    table = np.where(k == 0, one, table)
    table = np.where(k == 1, np.where(t % 2 == 0, one, -one), table)
    high = table.astype(ml_dtypes.bfloat16)
    low = (table - high.astype(np.float64)).astype(ml_dtypes.bfloat16)
    return high, low


def product(high, low, x):
    x_high = x.astype(jnp.bfloat16)
    x_low = (x - x_high.astype(jnp.float32)).astype(jnp.bfloat16)
    dot = functools.partial(jnp.dot, preferred_element_type=jnp.float32)
    return dot(high, x_high) + (dot(high, x_low) + dot(low, x_high))


def kernel(
    adj_hbm, state_hbm, wake_hbm, bh_hbm, bl_hbm, th_hbm, tl_hbm, ja_hbm, jr_hbm, js_hbm, wc_hbm,
    out_ref, grad_ref,
    adj_ref, state_ref, wake_ref, bh_ref, bl_ref, th_ref, tl_ref, ja_ref, jr_ref, js_ref, wc_ref, in_sem,
    send, recv, wsend, wrecv, wfull, back, ret, hsend, hrecv, esend, erecv, acc,
    f_ssem, f_rsem, w_ssem, w_rsem, b_ssem, b_rsem, h_ssem, h_rsem, e_ssem, e_rsem,
):
    me = lax.axis_index("mode")
    ax = lax.axis_index("ax")
    rad = lax.axis_index("rad")
    ax_count = lax.axis_size("ax")
    ax_up = lax.rem(ax + 1, ax_count)
    ax_down = lax.rem(ax + ax_count - 1, ax_count)
    others = [lax.rem(me + i, D) for i in ORDER]

    barrier = pltpu.get_barrier_semaphore()
    for other in others:
        pl.semaphore_signal(barrier, inc=1, device_id={"mode": other}, device_id_type=MESH)
    pl.semaphore_signal(barrier, inc=1, device_id={"ax": ax_up}, device_id_type=MESH)
    pl.semaphore_signal(barrier, inc=1, device_id={"ax": ax_down}, device_id_type=MESH)
    pl.semaphore_signal(barrier, inc=1, device_id={"rad": 1 - rad}, device_id_type=MESH)

    sources = (adj_hbm, state_hbm, wake_hbm, bh_hbm, bl_hbm, th_hbm, tl_hbm, ja_hbm, jr_hbm, js_hbm, wc_hbm)
    targets = (adj_ref, state_ref, wake_ref, bh_ref, bl_ref, th_ref, tl_ref, ja_ref, jr_ref, js_ref, wc_ref)
    loads = [pltpu.make_async_copy(a, b, in_sem.at[i]) for i, (a, b) in enumerate(zip(sources, targets))]
    for i in (10, 1, 0, 2, 3, 4, 5, 6, 7, 8, 9):
        loads[i].start()

    lane = lax.broadcasted_iota(jnp.int32, (K, L), 1)
    low_half = lane < HALF

    def cells(ref, f, x):
        return ref[f, pl.ds(x, K, stride=X), :]

    def swap(v):
        return pltpu.roll(v, HALF, axis=1)

    started = []

    def go(src, dst, ssem, rsem, device):
        copy = pltpu.make_async_remote_copy(
            src_ref=src, dst_ref=dst, send_sem=ssem, recv_sem=rsem, device_id=device, device_id_type=MESH
        )
        copy.start()
        started.append(copy)

    for i in (10, 1, 0):
        loads[i].wait()
    q = K // 2
    for f in range(F):
        for x in range(X):
            a = cells(adj_ref, f, x)
            c = wc_ref[f, 0] * cells(state_ref, 0, x)
            for e in range(1, F):
                c = c + wc_ref[f, e] * cells(state_ref, e, x)
            send[f, 2 * x] = jnp.where(low_half, a, swap(c))
            send[f, 2 * x + 1] = jnp.where(low_half, swap(a), c)
        if f == 0:
            loads[2].wait()
            for x in range(X):
                w = wake_ref[pl.ds(x, K, stride=X), :]
                w_swap = swap(w)
                m = low_half[:q]
                wsend[2 * x] = jnp.where(m, w[:q], w_swap[q:])
                wsend[2 * x + 1] = jnp.where(m, w_swap[:q], w[q:])
            pl.semaphore_wait(barrier, D + 2)
        for other in others:
            go(send.at[f, other], recv.at[f, me], f_ssem.at[f, other], f_rsem.at[f, me], {"mode": other})
        if f == 0:
            for other in others:
                go(wsend.at[other], wrecv.at[me], w_ssem.at[other], w_rsem.at[me], {"mode": other})

    edge = jnp.zeros((K, L), jnp.float32)
    for f in range(F):
        hsend[0, f] = cells(adj_ref, f, 0)
        hsend[1, f] = cells(adj_ref, f, X - 1)
        for x in range(X):
            s = f * X + x
            v = cells(adj_ref, f, x)
            v = jnp.where(rad == 0, pltpu.roll(v, s + 1, axis=1), pltpu.roll(v, s, axis=1) if s else v)
            edge = jnp.where(lane == s, v, edge)
    esend[...] = edge
    go(hsend.at[0], hrecv.at[1], h_ssem.at[0], h_rsem.at[1], {"ax": ax_down})
    go(hsend.at[1], hrecv.at[0], h_ssem.at[1], h_rsem.at[0], {"ax": ax_up})
    go(esend, erecv, e_ssem, e_rsem, {"rad": 1 - rad})

    wrecv[me] = wsend[me]
    for f in range(F):
        recv[f, me] = send[f, me]

    def arrived(ref, sem):
        pltpu.make_async_remote_copy(
            src_ref=ref, dst_ref=ref, send_sem=sem, recv_sem=sem, device_id={"mode": me}, device_id_type=MESH
        ).wait_recv()

    for other in others:
        arrived(wrecv.at[other], w_rsem.at[other])
    for d in range(D):
        w = wrecv[d]
        w_swap = swap(w)
        m = low_half[:q]
        wfull[pl.ds(d * K, q), :] = jnp.where(m, w, w_swap)
        wfull[pl.ds(d * K + q, q), :] = jnp.where(m, w_swap, w)

    for i in (3, 4, 5, 6, 7, 8, 9):
        loads[i].wait()
    low_all = lax.broadcasted_iota(jnp.int32, (D * K, L), 1) < HALF
    total = None
    first = None
    for f in range(F):
        for other in others:
            arrived(recv.at[f, other], f_rsem.at[f, other])
        angle = product(bh_ref[...], bl_ref[...], recv[f].reshape(D * K, L))
        angle_swap = swap(angle)
        term = angle * angle_swap
        total = term if total is None else total + term
        wake_all = wfull[...]
        if f % 2 == 0 and f < F - 1:
            first = wake_all * angle
            continue
        p = f // 2
        if f < F - 1:
            both = jnp.where(low_all, first, wake_all * angle_swap)
        else:
            both = wake_all * angle
        result = product(th_ref[...], tl_ref[...], both)
        if f == F - 1:
            result = jnp.where(low_all, result, -total)
        back[p] = result.reshape(D, K, L)
        for other in others:
            go(back.at[p, other], ret.at[p, me], b_ssem.at[p, other], b_rsem.at[p, me], {"mode": other})
        ret[p, me] = back[p, me]

    arrived(hrecv.at[0], h_rsem.at[0])
    arrived(hrecv.at[1], h_rsem.at[1])
    arrived(erecv, e_rsem)
    row = lax.broadcasted_iota(jnp.int32, (K, L), 0)
    even = lax.rem(row, 2) == 0
    order = lax.div(me * K + row, 2).astype(jnp.float32) / jnp.float32(D * K // 2)
    radius = 0.5 + ((rad * L + lane).astype(jnp.float32) + 0.5) / jnp.float32(4.0 * L)
    rate = (0.25 / radius) * order
    rate = jnp.where(even, rate, -rate)
    nearby = erecv[...]
    nearby_up = jnp.where(rad == 0, nearby, 0.0)
    nearby_down = jnp.where(rad == 1, nearby, 0.0)
    for x in range(X):
        fields, axial, radial, turned = [], [], [], []
        for e in range(F):
            a = cells(adj_ref, e, x)
            fields.append(a)
            if x == X - 1:
                above = jnp.where(ax < ax_count - 1, hrecv[1, e], 0.0)
            else:
                above = cells(adj_ref, e, x + 1)
            if x == 0:
                below = jnp.where(ax > 0, hrecv[0, e], 0.0)
            else:
                below = cells(adj_ref, e, x - 1)
            axial.append(0.5 * (above - below))
            s = e * X + x
            up = jnp.where(lane == L - 1, pltpu.roll(nearby_up, L - 1 - s, axis=1), pltpu.roll(a, L - 1, axis=1))
            edge_down = pltpu.roll(nearby_down, L - s, axis=1) if s else nearby_down
            down = jnp.where(lane == 0, edge_down, pltpu.roll(a, 1, axis=1))
            radial.append(0.5 * (up - down))
            turned.append(rate * jnp.where(even, pltpu.roll(a, K - 1, axis=0), pltpu.roll(a, 1, axis=0)))
        for f in range(F):
            v = fields[f]
            for e in range(F):
                v = v + ja_ref[e, f] * axial[e] + jr_ref[e, f] * radial[e] + js_ref[e, f] * turned[e]
            acc[f, x] = v

    for p in range(PAIRS):
        for other in others:
            arrived(ret.at[p, other], b_rsem.at[p, other])
    for x in range(X):
        returned = []
        for p in range(PAIRS):
            one, two = ret[p, 2 * x], ret[p, 2 * x + 1]
            returned.append(jnp.where(low_half, one, swap(two)))
            returned.append(jnp.where(low_half, swap(one), two))
        grad_ref[pl.ds(x, K, stride=X), :] = returned[F]
        for f in range(F):
            v = acc[f, x]
            for e in range(F):
                v = v - wc_ref[e, f] * returned[e]
            out_ref[f, pl.ds(x, K, stride=X), :] = v

    for copy in started:
        copy.wait_send()


def body(adjoint, state, wake, jac_axial, jac_radial, jac_swirl, wake_coupling):
    high, low = basis_parts()
    vmem = pl.BlockSpec(memory_space=pltpu.VMEM)
    hbm = pl.BlockSpec(memory_space=pltpu.HBM)
    dma = pltpu.SemaphoreType.DMA
    f32 = jnp.float32
    adjoint_in, grad = pl.pallas_call(
        kernel,
        out_shape=(
            jax.ShapeDtypeStruct((F, K * X, L), f32),
            jax.ShapeDtypeStruct((K * X, L), f32),
        ),
        in_specs=[hbm] * 11,
        out_specs=(vmem, vmem),
        scratch_shapes=[
            pltpu.VMEM((F, K * X, L), f32),
            pltpu.VMEM((F, K * X, L), f32),
            pltpu.VMEM((K * X, L), f32),
            *[pltpu.VMEM((D * K, D * K), jnp.bfloat16)] * 4,
            *[pltpu.SMEM((F, F), f32)] * 4,
            dma((11,)),
            pltpu.VMEM((F, D, K, L), f32),
            pltpu.VMEM((F, D, K, L), f32),
            pltpu.VMEM((D, K // 2, L), f32),
            pltpu.VMEM((D, K // 2, L), f32),
            pltpu.VMEM((D * K, L), f32),
            pltpu.VMEM((PAIRS, D, K, L), f32),
            pltpu.VMEM((PAIRS, D, K, L), f32),
            pltpu.VMEM((2, F, K, L), f32),
            pltpu.VMEM((2, F, K, L), f32),
            pltpu.VMEM((K, L), f32),
            pltpu.VMEM((K, L), f32),
            pltpu.VMEM((F, X, K, L), f32),
            dma((F, D)), dma((F, D)), dma((D,)), dma((D,)), dma((PAIRS, D)), dma((PAIRS, D)),
            dma((2,)), dma((2,)), dma, dma,
        ],
        compiler_params=pltpu.CompilerParams(
            collective_id=0, has_side_effects=True, vmem_limit_bytes=32 * 1024 * 1024
        ),
        name="section_adjoint",
    )(
        *[pltpu.with_memory_space_constraint(v, pltpu.HBM) for v in (adjoint.reshape(F, K * X, L), state.reshape(F, K * X, L), wake.reshape(K * X, L),
        jnp.asarray(high), jnp.asarray(low), jnp.asarray(np.ascontiguousarray(high.T)),
        jnp.asarray(np.ascontiguousarray(low.T)), jac_axial, jac_radial, jac_swirl, wake_coupling)],
    )
    return adjoint_in.reshape(adjoint.shape), grad.reshape(wake.shape)


def solution(mesh):
    return jax.shard_map(
        body,
        mesh=mesh,
        in_specs=(
            P(None, "mode", "ax", "rad"),
            P(None, "mode", "ax", "rad"),
            P("mode", "ax", "rad"),
            P(),
            P(),
            P(),
            P(),
        ),
        out_specs=(P(None, "mode", "ax", "rad"), P("mode", "ax", "rad")),
        check_vma=False,
    )
```

```python
import functools
import math

import jax
import jax.numpy as jnp
import ml_dtypes
import numpy as np
from jax import lax
from jax.experimental import pallas as pl
from jax.experimental.pallas import tpu as pltpu
from jax.sharding import PartitionSpec as P

MESH = pl.DeviceIdType.MESH
F, K, X, L = 5, 32, 4, 128
D = 8
HALF = L // 2
PAIRS = 3
ORDER = (4, 5, 3, 2, 6, 7, 1)


def basis_parts():
    t = np.arange(D * K)[:, None]
    k = np.arange(D * K)[None, :]
    phase = ((k // 2) * t % (D * K)) * (2.0 * math.pi / (D * K))
    table = math.sqrt(2.0 / (D * K)) * np.where(k % 2 == 0, np.cos(phase), np.sin(phase))
    one = 1.0 / math.sqrt(D * K)
    table = np.where(k == 0, one, table)
    table = np.where(k == 1, np.where(t % 2 == 0, one, -one), table)
    high = table.astype(ml_dtypes.bfloat16)
    low = (table - high.astype(np.float64)).astype(ml_dtypes.bfloat16)
    return high, low


def product(high, low, x):
    x_high = x.astype(jnp.bfloat16)
    x_low = (x - x_high.astype(jnp.float32)).astype(jnp.bfloat16)
    dot = functools.partial(jnp.dot, preferred_element_type=jnp.float32)
    return dot(high, x_high) + (dot(high, x_low) + dot(low, x_high))


def kernel(
    adj_hbm, state_hbm, wake_hbm, bh_hbm, bl_hbm, th_hbm, tl_hbm, ja_hbm, jr_hbm, js_hbm, wc_hbm,
    out_ref, grad_ref,
    adj_ref, state_ref, wake_ref, bh_ref, bl_ref, th_ref, tl_ref, ja_ref, jr_ref, js_ref, wc_ref, in_sem,
    send, recv, wsend, wrecv, wfull, back, ret, hsend, hrecv, esend, erecv, acc,
    f_ssem, f_rsem, w_ssem, w_rsem, b_ssem, b_rsem, h_ssem, h_rsem, e_ssem, e_rsem,
):
    me = lax.axis_index("mode")
    ax = lax.axis_index("ax")
    rad = lax.axis_index("rad")
    ax_count = lax.axis_size("ax")
    has_up = ax < ax_count - 1
    has_down = ax > 0
    others = [lax.rem(me + i, D) for i in ORDER]

    barrier = pltpu.get_barrier_semaphore()
    for other in others:
        pl.semaphore_signal(barrier, inc=1, device_id={"mode": other}, device_id_type=MESH)

    @pl.when(has_up)
    def _():
        pl.semaphore_signal(barrier, inc=1, device_id={"ax": ax + 1}, device_id_type=MESH)

    @pl.when(has_down)
    def _():
        pl.semaphore_signal(barrier, inc=1, device_id={"ax": ax - 1}, device_id_type=MESH)

    pl.semaphore_signal(barrier, inc=1, device_id={"rad": 1 - rad}, device_id_type=MESH)

    sources = (adj_hbm, state_hbm, wake_hbm, bh_hbm, bl_hbm, th_hbm, tl_hbm, ja_hbm, jr_hbm, js_hbm, wc_hbm)
    targets = (adj_ref, state_ref, wake_ref, bh_ref, bl_ref, th_ref, tl_ref, ja_ref, jr_ref, js_ref, wc_ref)
    loads = [pltpu.make_async_copy(a, b, in_sem.at[i]) for i, (a, b) in enumerate(zip(sources, targets))]
    for i in (10, 1, 0, 2, 3, 4, 5, 6, 7, 8, 9):
        loads[i].start()

    lane = lax.broadcasted_iota(jnp.int32, (K, L), 1)
    low_half = lane < HALF

    def cells(ref, f, x):
        return ref[f, pl.ds(x, K, stride=X), :]

    def swap(v):
        return pltpu.roll(v, HALF, axis=1)

    def go(src, dst, ssem, rsem, device):
        copy = pltpu.make_async_remote_copy(
            src_ref=src, dst_ref=dst, send_sem=ssem, recv_sem=rsem, device_id=device, device_id_type=MESH
        )
        copy.start()
        return copy

    for i in (10, 1, 0):
        loads[i].wait()
    q = K // 2
    for f in range(F):
        for x in range(X):
            a = cells(adj_ref, f, x)
            c = wc_ref[f, 0] * cells(state_ref, 0, x)
            for e in range(1, F):
                c = c + wc_ref[f, e] * cells(state_ref, e, x)
            send[f, 2 * x] = jnp.where(low_half, a, swap(c))
            send[f, 2 * x + 1] = jnp.where(low_half, swap(a), c)
        if f == 0:
            loads[2].wait()
            for x in range(X):
                w = wake_ref[pl.ds(x, K, stride=X), :]
                w_swap = swap(w)
                m = low_half[:q]
                wsend[2 * x] = jnp.where(m, w[:q], w_swap[q:])
                wsend[2 * x + 1] = jnp.where(m, w_swap[:q], w[q:])
            pl.semaphore_wait(barrier, D + has_up.astype(jnp.int32) + has_down.astype(jnp.int32))
        for other in others:
            go(send.at[f, other], recv.at[f, me], f_ssem.at[f], f_rsem.at[f], {"mode": other})
        if f == 0:
            for other in others:
                go(wsend.at[other], wrecv.at[me], w_ssem, w_rsem, {"mode": other})

    edge = jnp.zeros((K, L), jnp.float32)
    for f in range(F):
        hsend[0, f] = cells(adj_ref, f, 0)
        hsend[1, f] = cells(adj_ref, f, X - 1)
        for x in range(X):
            s = f * X + x
            v = cells(adj_ref, f, x)
            v = jnp.where(rad == 0, pltpu.roll(v, s + 1, axis=1), pltpu.roll(v, s, axis=1) if s else v)
            edge = jnp.where(lane == s, v, edge)
    esend[...] = edge

    @pl.when(has_down)
    def _():
        go(hsend.at[0], hrecv.at[1], h_ssem.at[0], h_rsem.at[1], {"ax": ax - 1})

    @pl.when(has_up)
    def _():
        go(hsend.at[1], hrecv.at[0], h_ssem.at[1], h_rsem.at[0], {"ax": ax + 1})

    go(esend, erecv, e_ssem, e_rsem, {"rad": 1 - rad})

    wrecv[me] = wsend[me]
    for f in range(F):
        recv[f, me] = send[f, me]

    def whole(ref, sem):
        return pltpu.make_async_remote_copy(
            src_ref=ref, dst_ref=ref, send_sem=sem, recv_sem=sem, device_id={"rad": 1 - rad}, device_id_type=MESH
        )

    seven = pl.ds(0, D - 1)

    whole(wrecv.at[seven], w_rsem).wait_recv()
    for d in range(D):
        w = wrecv[d]
        w_swap = swap(w)
        m = low_half[:q]
        wfull[pl.ds(d * K, q), :] = jnp.where(m, w, w_swap)
        wfull[pl.ds(d * K + q, q), :] = jnp.where(m, w_swap, w)

    for i in (3, 4, 5, 6, 7, 8, 9):
        loads[i].wait()
    low_all = lax.broadcasted_iota(jnp.int32, (D * K, L), 1) < HALF
    total = None
    first = None
    for f in range(F):
        whole(recv.at[f, seven], f_rsem.at[f]).wait_recv()
        angle = product(bh_ref[...], bl_ref[...], recv[f].reshape(D * K, L))
        angle_swap = swap(angle)
        term = angle * angle_swap
        total = term if total is None else total + term
        wake_all = wfull[...]
        if f % 2 == 0 and f < F - 1:
            first = wake_all * angle
            continue
        p = f // 2
        if f < F - 1:
            both = jnp.where(low_all, first, wake_all * angle_swap)
        else:
            both = wake_all * angle
        result = product(th_ref[...], tl_ref[...], both)
        if f == F - 1:
            result = jnp.where(low_all, result, -total)
        back[p] = result.reshape(D, K, L)
        for other in others:
            go(back.at[p, other], ret.at[p, me], b_ssem.at[p], b_rsem.at[p], {"mode": other})
        ret[p, me] = back[p, me]

    @pl.when(has_down)
    def _():
        whole(hrecv.at[0], h_rsem.at[0]).wait_recv()
        whole(hsend.at[0], h_ssem.at[0]).wait_send()

    @pl.when(has_up)
    def _():
        whole(hrecv.at[1], h_rsem.at[1]).wait_recv()
        whole(hsend.at[1], h_ssem.at[1]).wait_send()

    whole(erecv, e_rsem).wait_recv()
    whole(esend, e_ssem).wait_send()
    whole(wsend.at[seven], w_ssem).wait_send()
    for f in range(F):
        whole(send.at[f, seven], f_ssem.at[f]).wait_send()
    row = lax.broadcasted_iota(jnp.int32, (K, L), 0)
    even = lax.rem(row, 2) == 0
    order = lax.div(me * K + row, 2).astype(jnp.float32) / jnp.float32(D * K // 2)
    radius = 0.5 + ((rad * L + lane).astype(jnp.float32) + 0.5) / jnp.float32(4.0 * L)
    rate = (0.25 / radius) * order
    rate = jnp.where(even, rate, -rate)
    nearby = erecv[...]
    nearby_up = jnp.where(rad == 0, nearby, 0.0)
    nearby_down = jnp.where(rad == 1, nearby, 0.0)
    for x in range(X):
        fields, axial, radial, turned = [], [], [], []
        for e in range(F):
            a = cells(adj_ref, e, x)
            fields.append(a)
            if x == X - 1:
                above = jnp.where(has_up, hrecv[1, e], 0.0)
            else:
                above = cells(adj_ref, e, x + 1)
            if x == 0:
                below = jnp.where(has_down, hrecv[0, e], 0.0)
            else:
                below = cells(adj_ref, e, x - 1)
            axial.append(0.5 * (above - below))
            s = e * X + x
            up = jnp.where(lane == L - 1, pltpu.roll(nearby_up, L - 1 - s, axis=1), pltpu.roll(a, L - 1, axis=1))
            edge_down = pltpu.roll(nearby_down, L - s, axis=1) if s else nearby_down
            down = jnp.where(lane == 0, edge_down, pltpu.roll(a, 1, axis=1))
            radial.append(0.5 * (up - down))
            turned.append(rate * jnp.where(even, pltpu.roll(a, K - 1, axis=0), pltpu.roll(a, 1, axis=0)))
        for f in range(F):
            v = fields[f]
            for e in range(F):
                v = v + ja_ref[e, f] * axial[e] + jr_ref[e, f] * radial[e] + js_ref[e, f] * turned[e]
            acc[f, x] = v

    def pair(p, x):
        one, two = ret[p, 2 * x], ret[p, 2 * x + 1]
        return jnp.where(low_half, one, swap(two)), jnp.where(low_half, swap(one), two)

    for p in range(PAIRS - 1):
        whole(ret.at[p, seven], b_rsem.at[p]).wait_recv()
        whole(back.at[p, seven], b_ssem.at[p]).wait_send()
    for x in range(X):
        returned = [v for p in range(PAIRS - 1) for v in pair(p, x)]
        for f in range(F):
            v = acc[f, x]
            for e in range(F - 1):
                v = v - wc_ref[e, f] * returned[e]
            acc[f, x] = v
    p = PAIRS - 1
    whole(back.at[p, seven], b_ssem.at[p]).wait_send()
    whole(ret.at[p, seven], b_rsem.at[p]).wait_recv()
    for x in range(X):
        last, grad = pair(p, x)
        grad_ref[pl.ds(x, K, stride=X), :] = grad
        for f in range(F):
            out_ref[f, pl.ds(x, K, stride=X), :] = acc[f, x] - wc_ref[F - 1, f] * last


def write_out(field_ref, grad_ref, field_out, grad_out, sem):
    copies = [
        pltpu.make_async_copy(field_ref, field_out, sem.at[0]),
        pltpu.make_async_copy(grad_ref, grad_out, sem.at[1]),
    ]
    for copy in copies:
        copy.start()
    for copy in copies:
        copy.wait()


def body(adjoint, state, wake, jac_axial, jac_radial, jac_swirl, wake_coupling):
    high, low = basis_parts()
    vmem = pl.BlockSpec(memory_space=pltpu.VMEM)
    hbm = pl.BlockSpec(memory_space=pltpu.HBM)
    dma = pltpu.SemaphoreType.DMA
    f32 = jnp.float32
    adjoint_in, grad = pl.pallas_call(
        kernel,
        out_shape=(
            jax.ShapeDtypeStruct((F, K * X, L), f32),
            jax.ShapeDtypeStruct((K * X, L), f32),
        ),
        in_specs=[hbm] * 11,
        out_specs=(vmem, vmem),
        scratch_shapes=[
            pltpu.VMEM((F, K * X, L), f32),
            pltpu.VMEM((F, K * X, L), f32),
            pltpu.VMEM((K * X, L), f32),
            *[pltpu.VMEM((D * K, D * K), jnp.bfloat16)] * 4,
            *[pltpu.SMEM((F, F), f32)] * 4,
            dma((11,)),
            pltpu.VMEM((F, D, K, L), f32),
            pltpu.VMEM((F, D, K, L), f32),
            pltpu.VMEM((D, K // 2, L), f32),
            pltpu.VMEM((D, K // 2, L), f32),
            pltpu.VMEM((D * K, L), f32),
            pltpu.VMEM((PAIRS, D, K, L), f32),
            pltpu.VMEM((PAIRS, D, K, L), f32),
            pltpu.VMEM((2, F, K, L), f32),
            pltpu.VMEM((2, F, K, L), f32),
            pltpu.VMEM((K, L), f32),
            pltpu.VMEM((K, L), f32),
            pltpu.VMEM((F, X, K, L), f32),
            dma((F,)), dma((F,)), dma, dma, dma((PAIRS,)), dma((PAIRS,)),
            dma((2,)), dma((2,)), dma, dma,
        ],
        compiler_params=pltpu.CompilerParams(
            collective_id=0, has_side_effects=True, vmem_limit_bytes=32 * 1024 * 1024
        ),
        name="section_adjoint",
    )(
        *[pltpu.with_memory_space_constraint(v, pltpu.HBM) for v in (adjoint.reshape(F, K * X, L), state.reshape(F, K * X, L), wake.reshape(K * X, L),
        jnp.asarray(high), jnp.asarray(low), jnp.asarray(np.ascontiguousarray(high.T)),
        jnp.asarray(np.ascontiguousarray(low.T)), jac_axial, jac_radial, jac_swirl, wake_coupling)],
    )
    adjoint_in, grad = pl.pallas_call(
        write_out,
        out_shape=(
            jax.ShapeDtypeStruct((F, K * X, L), f32),
            jax.ShapeDtypeStruct((K * X, L), f32),
        ),
        in_specs=[vmem] * 2,
        out_specs=(hbm, hbm),
        scratch_shapes=[dma((2,))],
        compiler_params=pltpu.CompilerParams(vmem_limit_bytes=1024 * 1024),
        name="write_out",
    )(adjoint_in, grad)
    return adjoint_in.reshape(adjoint.shape), grad.reshape(wake.shape)


def solution(mesh):
    return jax.shard_map(
        body,
        mesh=mesh,
        in_specs=(
            P(None, "mode", "ax", "rad"),
            P(None, "mode", "ax", "rad"),
            P("mode", "ax", "rad"),
            P(),
            P(),
            P(),
            P(),
        ),
        out_specs=(P(None, "mode", "ax", "rad"), P("mode", "ax", "rad")),
        check_vma=False,
    )
```

```python
import functools
import math

import jax
import jax.numpy as jnp
import ml_dtypes
import numpy as np
from jax import lax
from jax.experimental import pallas as pl
from jax.experimental.pallas import tpu as pltpu
from jax.sharding import PartitionSpec as P

MESH = pl.DeviceIdType.MESH
F, K, X, L = 5, 32, 4, 128
D = 8
HALF = L // 2
PAIRS = 3
ORDER = (4, 5, 3, 2, 6, 7, 1)


def basis_parts():
    t = np.arange(D * K)[:, None]
    k = np.arange(D * K)[None, :]
    phase = ((k // 2) * t % (D * K)) * (2.0 * math.pi / (D * K))
    table = math.sqrt(2.0 / (D * K)) * np.where(k % 2 == 0, np.cos(phase), np.sin(phase))
    one = 1.0 / math.sqrt(D * K)
    table = np.where(k == 0, one, table)
    table = np.where(k == 1, np.where(t % 2 == 0, one, -one), table)
    high = table.astype(ml_dtypes.bfloat16)
    low = (table - high.astype(np.float64)).astype(ml_dtypes.bfloat16)
    return high, low


def product(high, low, x):
    x_high = x.astype(jnp.bfloat16)
    x_low = (x - x_high.astype(jnp.float32)).astype(jnp.bfloat16)
    dot = functools.partial(jnp.dot, preferred_element_type=jnp.float32)
    return dot(high, x_high) + (dot(high, x_low) + dot(low, x_high))


def kernel(
    adj_hbm, state_hbm, wake_hbm, bh_hbm, bl_hbm, th_hbm, tl_hbm, ja_hbm, jr_hbm, js_hbm, wc_hbm,
    out_ref, grad_ref,
    adj_ref, state_ref, wake_ref, bh_ref, bl_ref, th_ref, tl_ref, ja_ref, jr_ref, js_ref, wc_ref, in_sem,
    send, recv, wsend, wrecv, wfull, back, ret, hsend, hrecv, esend, erecv, acc,
    f_ssem, f_rsem, w_ssem, w_rsem, b_ssem, b_rsem, h_ssem, h_rsem, e_ssem, e_rsem, group_sem, near_sem,
):
    me = lax.axis_index("mode")
    ax = lax.axis_index("ax")
    rad = lax.axis_index("rad")
    ax_count = lax.axis_size("ax")
    has_up = ax < ax_count - 1
    has_down = ax > 0
    others = [lax.rem(me + i, D) for i in ORDER]

    barrier = pltpu.get_barrier_semaphore()
    host = me == D - 1
    for other in others:

        @pl.when(other != D - 1)
        def _():
            pl.semaphore_signal(barrier, inc=1, device_id={"mode": other}, device_id_type=MESH)

    sources = (adj_hbm, state_hbm, wake_hbm, bh_hbm, bl_hbm, th_hbm, tl_hbm, ja_hbm, jr_hbm, js_hbm, wc_hbm)
    targets = (adj_ref, state_ref, wake_ref, bh_ref, bl_ref, th_ref, tl_ref, ja_ref, jr_ref, js_ref, wc_ref)
    loads = [pltpu.make_async_copy(a, b, in_sem.at[i]) for i, (a, b) in enumerate(zip(sources, targets))]
    for i in (10, 1, 0, 2, 3, 4, 5, 6, 7, 8, 9):
        loads[i].start()

    lane = lax.broadcasted_iota(jnp.int32, (K, L), 1)
    low_half = lane < HALF

    def cells(ref, f, x):
        return ref[f, pl.ds(x, K, stride=X), :]

    def swap(v):
        return pltpu.roll(v, HALF, axis=1)

    def go(src, dst, ssem, rsem, device):
        copy = pltpu.make_async_remote_copy(
            src_ref=src, dst_ref=dst, send_sem=ssem, recv_sem=rsem, device_id=device, device_id_type=MESH
        )
        copy.start()
        return copy

    for i in (10, 1, 0):
        loads[i].wait()
    q = K // 2
    for f in range(F):
        for x in range(X):
            a = cells(adj_ref, f, x)
            c = wc_ref[f, 0] * cells(state_ref, 0, x)
            for e in range(1, F):
                c = c + wc_ref[f, e] * cells(state_ref, e, x)
            send[f, 2 * x] = jnp.where(low_half, a, swap(c))
            send[f, 2 * x + 1] = jnp.where(low_half, swap(a), c)
        if f == 0:
            loads[2].wait()
            for x in range(X):
                w = wake_ref[pl.ds(x, K, stride=X), :]
                w_swap = swap(w)
                m = low_half[:q]
                wsend[2 * x] = jnp.where(m, w[:q], w_swap[q:])
                wsend[2 * x + 1] = jnp.where(m, w_swap[:q], w[q:])

            @pl.when(jnp.logical_not(host))
            def _():
                pl.semaphore_wait(barrier, D - 1)

            @pl.when(me == D - 2)
            def _():
                pl.semaphore_signal(group_sem, inc=1, device_id={"mode": me + 1}, device_id_type=MESH)

            @pl.when(host)
            def _():
                pl.semaphore_wait(group_sem, 1)

        for other in others:
            go(send.at[f, other], recv.at[f, me], f_ssem.at[f], f_rsem.at[f], {"mode": other})
        if f == 0:
            for other in others:
                go(wsend.at[other], wrecv.at[me], w_ssem, w_rsem, {"mode": other})

    edge = jnp.zeros((K, L), jnp.float32)
    for f in range(F):
        hsend[0, f] = cells(adj_ref, f, 0)
        hsend[1, f] = cells(adj_ref, f, X - 1)
        for x in range(X):
            s = f * X + x
            v = cells(adj_ref, f, x)
            v = jnp.where(rad == 0, pltpu.roll(v, s + 1, axis=1), pltpu.roll(v, s, axis=1) if s else v)
            edge = jnp.where(lane == s, v, edge)
    esend[...] = edge

    @pl.when(host)
    def _():
        pl.semaphore_signal(barrier, inc=1, device_id={"rad": 1 - rad}, device_id_type=MESH)

    @pl.when(jnp.logical_and(host, has_up))
    def _():
        pl.semaphore_signal(barrier, inc=1, device_id={"ax": ax + 1}, device_id_type=MESH)

    @pl.when(jnp.logical_and(host, has_down))
    def _():
        pl.semaphore_signal(barrier, inc=1, device_id={"ax": ax - 1}, device_id_type=MESH)

    def tell_group():
        @pl.when(host)
        def _():
            pl.semaphore_wait(barrier, 1 + has_up.astype(jnp.int32) + has_down.astype(jnp.int32))
            for other in range(D - 1):
                pl.semaphore_signal(near_sem, inc=1, device_id={"mode": other}, device_id_type=MESH)

    def send_halos():
        @pl.when(jnp.logical_not(host))
        def _():
            pl.semaphore_wait(near_sem, 1)

        @pl.when(has_down)
        def _():
            go(hsend.at[0], hrecv.at[1], h_ssem.at[0], h_rsem.at[1], {"ax": ax - 1})

        @pl.when(has_up)
        def _():
            go(hsend.at[1], hrecv.at[0], h_ssem.at[1], h_rsem.at[0], {"ax": ax + 1})

        go(esend, erecv, e_ssem, e_rsem, {"rad": 1 - rad})

    wrecv[me] = wsend[me]
    for f in range(F):
        recv[f, me] = send[f, me]

    def whole(ref, sem):
        return pltpu.make_async_remote_copy(
            src_ref=ref, dst_ref=ref, send_sem=sem, recv_sem=sem, device_id={"rad": 1 - rad}, device_id_type=MESH
        )

    seven = pl.ds(0, D - 1)

    whole(wrecv.at[seven], w_rsem).wait_recv()
    for d in range(D):
        w = wrecv[d]
        w_swap = swap(w)
        m = low_half[:q]
        wfull[pl.ds(d * K, q), :] = jnp.where(m, w, w_swap)
        wfull[pl.ds(d * K + q, q), :] = jnp.where(m, w_swap, w)

    for i in (3, 4, 5, 6, 7, 8, 9):
        loads[i].wait()
    low_all = lax.broadcasted_iota(jnp.int32, (D * K, L), 1) < HALF
    total = None
    first = None
    for f in range(F):
        if f == F - 2:
            tell_group()
        if f == F - 1:
            send_halos()
        whole(recv.at[f, seven], f_rsem.at[f]).wait_recv()
        angle = product(bh_ref[...], bl_ref[...], recv[f].reshape(D * K, L))
        angle_swap = swap(angle)
        term = angle * angle_swap
        total = term if total is None else total + term
        wake_all = wfull[...]
        if f % 2 == 0 and f < F - 1:
            first = wake_all * angle
            continue
        p = f // 2
        if f < F - 1:
            both = jnp.where(low_all, first, wake_all * angle_swap)
        else:
            both = wake_all * angle
        result = product(th_ref[...], tl_ref[...], both)
        if f == F - 1:
            result = jnp.where(low_all, result, -total)
        back[p] = result.reshape(D, K, L)
        for other in others:
            go(back.at[p, other], ret.at[p, me], b_ssem.at[p], b_rsem.at[p], {"mode": other})
        ret[p, me] = back[p, me]

    @pl.when(has_down)
    def _():
        whole(hrecv.at[0], h_rsem.at[0]).wait_recv()
        whole(hsend.at[0], h_ssem.at[0]).wait_send()

    @pl.when(has_up)
    def _():
        whole(hrecv.at[1], h_rsem.at[1]).wait_recv()
        whole(hsend.at[1], h_ssem.at[1]).wait_send()

    whole(erecv, e_rsem).wait_recv()
    whole(esend, e_ssem).wait_send()
    whole(wsend.at[seven], w_ssem).wait_send()
    for f in range(F):
        whole(send.at[f, seven], f_ssem.at[f]).wait_send()
    row = lax.broadcasted_iota(jnp.int32, (K, L), 0)
    even = lax.rem(row, 2) == 0
    order = lax.div(me * K + row, 2).astype(jnp.float32) / jnp.float32(D * K // 2)
    radius = 0.5 + ((rad * L + lane).astype(jnp.float32) + 0.5) / jnp.float32(4.0 * L)
    rate = (0.25 / radius) * order
    rate = jnp.where(even, rate, -rate)
    nearby = erecv[...]
    nearby_up = jnp.where(rad == 0, nearby, 0.0)
    nearby_down = jnp.where(rad == 1, nearby, 0.0)
    for x in range(X):
        fields, axial, radial, turned = [], [], [], []
        for e in range(F):
            a = cells(adj_ref, e, x)
            fields.append(a)
            if x == X - 1:
                above = jnp.where(has_up, hrecv[1, e], 0.0)
            else:
                above = cells(adj_ref, e, x + 1)
            if x == 0:
                below = jnp.where(has_down, hrecv[0, e], 0.0)
            else:
                below = cells(adj_ref, e, x - 1)
            axial.append(0.5 * (above - below))
            s = e * X + x
            up = jnp.where(lane == L - 1, pltpu.roll(nearby_up, L - 1 - s, axis=1), pltpu.roll(a, L - 1, axis=1))
            edge_down = pltpu.roll(nearby_down, L - s, axis=1) if s else nearby_down
            down = jnp.where(lane == 0, edge_down, pltpu.roll(a, 1, axis=1))
            radial.append(0.5 * (up - down))
            turned.append(rate * jnp.where(even, pltpu.roll(a, K - 1, axis=0), pltpu.roll(a, 1, axis=0)))
        for f in range(F):
            v = fields[f]
            for e in range(F):
                v = v + ja_ref[e, f] * axial[e] + jr_ref[e, f] * radial[e] + js_ref[e, f] * turned[e]
            acc[f, x] = v

    def pair(p, x):
        one, two = ret[p, 2 * x], ret[p, 2 * x + 1]
        return jnp.where(low_half, one, swap(two)), jnp.where(low_half, swap(one), two)

    for p in range(PAIRS - 1):
        whole(ret.at[p, seven], b_rsem.at[p]).wait_recv()
        whole(back.at[p, seven], b_ssem.at[p]).wait_send()
    for x in range(X):
        returned = [v for p in range(PAIRS - 1) for v in pair(p, x)]
        for f in range(F):
            v = acc[f, x]
            for e in range(F - 1):
                v = v - wc_ref[e, f] * returned[e]
            acc[f, x] = v
    p = PAIRS - 1
    whole(back.at[p, seven], b_ssem.at[p]).wait_send()
    whole(ret.at[p, seven], b_rsem.at[p]).wait_recv()
    for x in range(X):
        last, grad = pair(p, x)
        grad_ref[pl.ds(x, K, stride=X), :] = grad
        for f in range(F):
            out_ref[f, pl.ds(x, K, stride=X), :] = acc[f, x] - wc_ref[F - 1, f] * last


def write_out(field_ref, grad_ref, field_out, grad_out, sem):
    copies = [
        pltpu.make_async_copy(field_ref, field_out, sem.at[0]),
        pltpu.make_async_copy(grad_ref, grad_out, sem.at[1]),
    ]
    for copy in copies:
        copy.start()
    for copy in copies:
        copy.wait()


def body(adjoint, state, wake, jac_axial, jac_radial, jac_swirl, wake_coupling):
    high, low = basis_parts()
    vmem = pl.BlockSpec(memory_space=pltpu.VMEM)
    hbm = pl.BlockSpec(memory_space=pltpu.HBM)
    dma = pltpu.SemaphoreType.DMA
    f32 = jnp.float32
    adjoint_in, grad = pl.pallas_call(
        kernel,
        out_shape=(
            jax.ShapeDtypeStruct((F, K * X, L), f32),
            jax.ShapeDtypeStruct((K * X, L), f32),
        ),
        in_specs=[hbm] * 11,
        out_specs=(vmem, vmem),
        scratch_shapes=[
            pltpu.VMEM((F, K * X, L), f32),
            pltpu.VMEM((F, K * X, L), f32),
            pltpu.VMEM((K * X, L), f32),
            *[pltpu.VMEM((D * K, D * K), jnp.bfloat16)] * 4,
            *[pltpu.SMEM((F, F), f32)] * 4,
            dma((11,)),
            pltpu.VMEM((F, D, K, L), f32),
            pltpu.VMEM((F, D, K, L), f32),
            pltpu.VMEM((D, K // 2, L), f32),
            pltpu.VMEM((D, K // 2, L), f32),
            pltpu.VMEM((D * K, L), f32),
            pltpu.VMEM((PAIRS, D, K, L), f32),
            pltpu.VMEM((PAIRS, D, K, L), f32),
            pltpu.VMEM((2, F, K, L), f32),
            pltpu.VMEM((2, F, K, L), f32),
            pltpu.VMEM((K, L), f32),
            pltpu.VMEM((K, L), f32),
            pltpu.VMEM((F, X, K, L), f32),
            dma((F,)), dma((F,)), dma, dma, dma((PAIRS,)), dma((PAIRS,)),
            dma((2,)), dma((2,)), dma, dma, pltpu.SemaphoreType.REGULAR, pltpu.SemaphoreType.REGULAR,
        ],
        compiler_params=pltpu.CompilerParams(
            collective_id=0, has_side_effects=True, vmem_limit_bytes=32 * 1024 * 1024
        ),
        name="section_adjoint",
    )(
        *[pltpu.with_memory_space_constraint(v, pltpu.HBM) for v in (adjoint.reshape(F, K * X, L), state.reshape(F, K * X, L), wake.reshape(K * X, L),
        jnp.asarray(high), jnp.asarray(low), jnp.asarray(np.ascontiguousarray(high.T)),
        jnp.asarray(np.ascontiguousarray(low.T)), jac_axial, jac_radial, jac_swirl, wake_coupling)],
    )
    adjoint_in, grad = pl.pallas_call(
        write_out,
        out_shape=(
            jax.ShapeDtypeStruct((F, K * X, L), f32),
            jax.ShapeDtypeStruct((K * X, L), f32),
        ),
        in_specs=[vmem] * 2,
        out_specs=(hbm, hbm),
        scratch_shapes=[dma((2,))],
        compiler_params=pltpu.CompilerParams(vmem_limit_bytes=1024 * 1024),
        name="write_out",
    )(adjoint_in, grad)
    return adjoint_in.reshape(adjoint.shape), grad.reshape(wake.shape)


def solution(mesh):
    return jax.shard_map(
        body,
        mesh=mesh,
        in_specs=(
            P(None, "mode", "ax", "rad"),
            P(None, "mode", "ax", "rad"),
            P("mode", "ax", "rad"),
            P(),
            P(),
            P(),
            P(),
        ),
        out_specs=(P(None, "mode", "ax", "rad"), P("mode", "ax", "rad")),
        check_vma=False,
    )
```

```python
import functools
import math

import jax
import jax.numpy as jnp
import ml_dtypes
import numpy as np
from jax import lax
from jax.experimental import pallas as pl
from jax.experimental.pallas import tpu as pltpu
from jax.sharding import PartitionSpec as P

MESH = pl.DeviceIdType.MESH
F, K, X, L = 5, 32, 4, 128
D = 8
HALF = L // 2
PAIRS = 3
ORDER = (4, 5, 3, 2, 6, 7, 1)


def basis_parts():
    t = np.arange(D * K)[:, None]
    k = np.arange(D * K)[None, :]
    phase = ((k // 2) * t % (D * K)) * (2.0 * math.pi / (D * K))
    table = math.sqrt(2.0 / (D * K)) * np.where(k % 2 == 0, np.cos(phase), np.sin(phase))
    one = 1.0 / math.sqrt(D * K)
    table = np.where(k == 0, one, table)
    table = np.where(k == 1, np.where(t % 2 == 0, one, -one), table)
    high = table.astype(ml_dtypes.bfloat16)
    low = (table - high.astype(np.float64)).astype(ml_dtypes.bfloat16)
    return high, low


def product(high, low, x):
    x_high = x.astype(jnp.bfloat16)
    x_low = (x - x_high.astype(jnp.float32)).astype(jnp.bfloat16)
    dot = functools.partial(jnp.dot, preferred_element_type=jnp.float32)
    return dot(high, x_high) + (dot(high, x_low) + dot(low, x_high))


def kernel(
    adj_hbm, state_hbm, wake_hbm, bh_hbm, bl_hbm, th_hbm, tl_hbm, ja_hbm, jr_hbm, js_hbm, wc_hbm,
    out_ref, grad_ref,
    adj_ref, state_ref, wake_ref, bh_ref, bl_ref, th_ref, tl_ref, ja_ref, jr_ref, js_ref, wc_ref, in_sem,
    send, recv, wsend, wrecv, wfull, back, ret, hsend, hrecv, esend, erecv, acc,
    f_ssem, f_rsem, w_ssem, w_rsem, b_ssem, b_rsem, h_ssem, h_rsem, e_ssem, e_rsem,
    relay, brelay, r_rsem, br_rsem, fw_ssem, fb_ssem,
):
    me = lax.axis_index("mode")
    ax = lax.axis_index("ax")
    rad = lax.axis_index("rad")
    ax_count = lax.axis_size("ax")
    has_up = ax < ax_count - 1
    has_down = ax > 0
    others = [lax.rem(me + i, D) for i in ORDER]
    core = lax.rem(me, 2)
    ahead = lax.rem(me - core + 2, D)
    behind = lax.rem(me - core + D - 2, D)
    away = lax.rem(me - core + 4, D)
    direct = [ahead + core, behind + core, ahead + 1 - core, behind + 1 - core, me + 1 - 2 * core]

    barrier = pltpu.get_barrier_semaphore()
    for other in others:
        pl.semaphore_signal(barrier, inc=1, device_id={"mode": other}, device_id_type=MESH)

    @pl.when(has_up)
    def _():
        pl.semaphore_signal(barrier, inc=1, device_id={"ax": ax + 1}, device_id_type=MESH)

    @pl.when(has_down)
    def _():
        pl.semaphore_signal(barrier, inc=1, device_id={"ax": ax - 1}, device_id_type=MESH)

    pl.semaphore_signal(barrier, inc=1, device_id={"rad": 1 - rad}, device_id_type=MESH)

    sources = (adj_hbm, state_hbm, wake_hbm, bh_hbm, bl_hbm, th_hbm, tl_hbm, ja_hbm, jr_hbm, js_hbm, wc_hbm)
    targets = (adj_ref, state_ref, wake_ref, bh_ref, bl_ref, th_ref, tl_ref, ja_ref, jr_ref, js_ref, wc_ref)
    loads = [pltpu.make_async_copy(a, b, in_sem.at[i]) for i, (a, b) in enumerate(zip(sources, targets))]
    for i in (10, 1, 0, 2, 3, 4, 5, 6, 7, 8, 9):
        loads[i].start()

    lane = lax.broadcasted_iota(jnp.int32, (K, L), 1)
    low_half = lane < HALF

    def cells(ref, f, x):
        return ref[f, pl.ds(x, K, stride=X), :]

    def swap(v):
        return pltpu.roll(v, HALF, axis=1)

    def go(src, dst, ssem, rsem, device):
        copy = pltpu.make_async_remote_copy(
            src_ref=src, dst_ref=dst, send_sem=ssem, recv_sem=rsem, device_id=device, device_id_type=MESH
        )
        copy.start()
        return copy

    def whole(ref, sem):
        return pltpu.make_async_remote_copy(
            src_ref=ref, dst_ref=ref, send_sem=sem, recv_sem=sem, device_id={"rad": 1 - rad}, device_id_type=MESH
        )

    def to_relay(src, dst, ssem, rsem):
        go(src.at[away], dst.at[0], ssem, rsem, {"mode": ahead + core})
        go(src.at[away + 1], dst.at[1], ssem, rsem, {"mode": behind + core})

    def to_near(src, dst, ssem, rsem):
        for other in direct:
            go(src.at[other], dst.at[me], ssem, rsem, {"mode": other})

    def forward(src, dst, arrival, ssem, rsem):
        whole(src, arrival).wait_recv()
        go(src.at[0], dst.at[behind + core], ssem, rsem, {"mode": ahead})
        go(src.at[1], dst.at[ahead + core], ssem, rsem, {"mode": behind + 1})

    for i in (10, 1, 0):
        loads[i].wait()
    q = K // 2
    for f in range(F):
        for x in range(X):
            a = cells(adj_ref, f, x)
            c = wc_ref[f, 0] * cells(state_ref, 0, x)
            for e in range(1, F):
                c = c + wc_ref[f, e] * cells(state_ref, e, x)
            send[f, 2 * x] = jnp.where(low_half, a, swap(c))
            send[f, 2 * x + 1] = jnp.where(low_half, swap(a), c)
        if f == 0:
            loads[2].wait()
            for x in range(X):
                w = wake_ref[pl.ds(x, K, stride=X), :]
                w_swap = swap(w)
                m = low_half[:q]
                wsend[2 * x] = jnp.where(m, w[:q], w_swap[q:])
                wsend[2 * x + 1] = jnp.where(m, w_swap[:q], w[q:])
            pl.semaphore_wait(barrier, D + has_up.astype(jnp.int32) + has_down.astype(jnp.int32))
        to_relay(send.at[f], relay.at[f], f_ssem.at[f], r_rsem.at[f])
        if f == 0:
            to_near(send.at[f], recv.at[f], f_ssem.at[f], f_rsem.at[f])
            for other in others:
                go(wsend.at[other], wrecv.at[me], w_ssem, w_rsem, {"mode": other})

    edge = jnp.zeros((K, L), jnp.float32)
    for f in range(F):
        hsend[0, f] = cells(adj_ref, f, 0)
        hsend[1, f] = cells(adj_ref, f, X - 1)
        for x in range(X):
            s = f * X + x
            v = cells(adj_ref, f, x)
            v = jnp.where(rad == 0, pltpu.roll(v, s + 1, axis=1), pltpu.roll(v, s, axis=1) if s else v)
            edge = jnp.where(lane == s, v, edge)
    esend[...] = edge

    @pl.when(has_down)
    def _():
        go(hsend.at[0], hrecv.at[1], h_ssem.at[0], h_rsem.at[1], {"ax": ax - 1})

    @pl.when(has_up)
    def _():
        go(hsend.at[1], hrecv.at[0], h_ssem.at[1], h_rsem.at[0], {"ax": ax + 1})

    go(esend, erecv, e_ssem, e_rsem, {"rad": 1 - rad})

    for f in range(F):
        forward(relay.at[f], recv.at[f], r_rsem.at[f], fw_ssem, f_rsem.at[f])
        if f < F - 1:
            to_near(send.at[f + 1], recv.at[f + 1], f_ssem.at[f + 1], f_rsem.at[f + 1])

    wrecv[me] = wsend[me]
    for f in range(F):
        recv[f, me] = send[f, me]

    seven = pl.ds(0, D - 1)

    whole(wrecv.at[seven], w_rsem).wait_recv()
    for d in range(D):
        w = wrecv[d]
        w_swap = swap(w)
        m = low_half[:q]
        wfull[pl.ds(d * K, q), :] = jnp.where(m, w, w_swap)
        wfull[pl.ds(d * K + q, q), :] = jnp.where(m, w_swap, w)

    for i in (3, 4, 5, 6, 7, 8, 9):
        loads[i].wait()
    def forward_back(p):
        forward(brelay.at[p], ret.at[p], br_rsem.at[p], fb_ssem, b_rsem.at[p])

    low_all = lax.broadcasted_iota(jnp.int32, (D * K, L), 1) < HALF
    total = None
    first = None
    for f in range(F):
        whole(recv.at[f, seven], f_rsem.at[f]).wait_recv()
        angle = product(bh_ref[...], bl_ref[...], recv[f].reshape(D * K, L))
        angle_swap = swap(angle)
        term = angle * angle_swap
        total = term if total is None else total + term
        wake_all = wfull[...]
        if f % 2 == 0 and f < F - 1:
            first = wake_all * angle
            continue
        p = f // 2
        if f < F - 1:
            both = jnp.where(low_all, first, wake_all * angle_swap)
        else:
            both = wake_all * angle
        result = product(th_ref[...], tl_ref[...], both)
        if f == F - 1:
            result = jnp.where(low_all, result, -total)
        back[p] = result.reshape(D, K, L)
        to_relay(back.at[p], brelay.at[p], b_ssem.at[p], br_rsem.at[p])
        to_near(back.at[p], ret.at[p], b_ssem.at[p], b_rsem.at[p])
        if p:
            forward_back(p - 1)
        ret[p, me] = back[p, me]

    @pl.when(has_down)
    def _():
        whole(hrecv.at[0], h_rsem.at[0]).wait_recv()
        whole(hsend.at[0], h_ssem.at[0]).wait_send()

    @pl.when(has_up)
    def _():
        whole(hrecv.at[1], h_rsem.at[1]).wait_recv()
        whole(hsend.at[1], h_ssem.at[1]).wait_send()

    whole(erecv, e_rsem).wait_recv()
    whole(esend, e_ssem).wait_send()
    whole(wsend.at[seven], w_ssem).wait_send()
    for f in range(F):
        whole(send.at[f, seven], f_ssem.at[f]).wait_send()
    row = lax.broadcasted_iota(jnp.int32, (K, L), 0)
    even = lax.rem(row, 2) == 0
    order = lax.div(me * K + row, 2).astype(jnp.float32) / jnp.float32(D * K // 2)
    radius = 0.5 + ((rad * L + lane).astype(jnp.float32) + 0.5) / jnp.float32(4.0 * L)
    rate = (0.25 / radius) * order
    rate = jnp.where(even, rate, -rate)
    nearby = erecv[...]
    nearby_up = jnp.where(rad == 0, nearby, 0.0)
    nearby_down = jnp.where(rad == 1, nearby, 0.0)
    for x in range(X):
        fields, axial, radial, turned = [], [], [], []
        for e in range(F):
            a = cells(adj_ref, e, x)
            fields.append(a)
            if x == X - 1:
                above = jnp.where(has_up, hrecv[1, e], 0.0)
            else:
                above = cells(adj_ref, e, x + 1)
            if x == 0:
                below = jnp.where(has_down, hrecv[0, e], 0.0)
            else:
                below = cells(adj_ref, e, x - 1)
            axial.append(0.5 * (above - below))
            s = e * X + x
            up = jnp.where(lane == L - 1, pltpu.roll(nearby_up, L - 1 - s, axis=1), pltpu.roll(a, L - 1, axis=1))
            edge_down = pltpu.roll(nearby_down, L - s, axis=1) if s else nearby_down
            down = jnp.where(lane == 0, edge_down, pltpu.roll(a, 1, axis=1))
            radial.append(0.5 * (up - down))
            turned.append(rate * jnp.where(even, pltpu.roll(a, K - 1, axis=0), pltpu.roll(a, 1, axis=0)))
        for f in range(F):
            v = fields[f]
            for e in range(F):
                v = v + ja_ref[e, f] * axial[e] + jr_ref[e, f] * radial[e] + js_ref[e, f] * turned[e]
            acc[f, x] = v

    forward_back(PAIRS - 1)
    whole(relay, fw_ssem).wait_send()

    def pair(p, x):
        one, two = ret[p, 2 * x], ret[p, 2 * x + 1]
        return jnp.where(low_half, one, swap(two)), jnp.where(low_half, swap(one), two)

    for p in range(PAIRS - 1):
        whole(ret.at[p, seven], b_rsem.at[p]).wait_recv()
        whole(back.at[p, seven], b_ssem.at[p]).wait_send()
    for x in range(X):
        returned = [v for p in range(PAIRS - 1) for v in pair(p, x)]
        for f in range(F):
            v = acc[f, x]
            for e in range(F - 1):
                v = v - wc_ref[e, f] * returned[e]
            acc[f, x] = v
    p = PAIRS - 1
    whole(brelay, fb_ssem).wait_send()
    whole(back.at[p, seven], b_ssem.at[p]).wait_send()
    whole(ret.at[p, seven], b_rsem.at[p]).wait_recv()
    for x in range(X):
        last, grad = pair(p, x)
        grad_ref[pl.ds(x, K, stride=X), :] = grad
        for f in range(F):
            out_ref[f, pl.ds(x, K, stride=X), :] = acc[f, x] - wc_ref[F - 1, f] * last


def write_out(field_ref, grad_ref, field_out, grad_out, sem):
    copies = [
        pltpu.make_async_copy(field_ref, field_out, sem.at[0]),
        pltpu.make_async_copy(grad_ref, grad_out, sem.at[1]),
    ]
    for copy in copies:
        copy.start()
    for copy in copies:
        copy.wait()


def body(adjoint, state, wake, jac_axial, jac_radial, jac_swirl, wake_coupling):
    high, low = basis_parts()
    vmem = pl.BlockSpec(memory_space=pltpu.VMEM)
    hbm = pl.BlockSpec(memory_space=pltpu.HBM)
    dma = pltpu.SemaphoreType.DMA
    f32 = jnp.float32
    adjoint_in, grad = pl.pallas_call(
        kernel,
        out_shape=(
            jax.ShapeDtypeStruct((F, K * X, L), f32),
            jax.ShapeDtypeStruct((K * X, L), f32),
        ),
        in_specs=[hbm] * 11,
        out_specs=(vmem, vmem),
        scratch_shapes=[
            pltpu.VMEM((F, K * X, L), f32),
            pltpu.VMEM((F, K * X, L), f32),
            pltpu.VMEM((K * X, L), f32),
            *[pltpu.VMEM((D * K, D * K), jnp.bfloat16)] * 4,
            *[pltpu.SMEM((F, F), f32)] * 4,
            dma((11,)),
            pltpu.VMEM((F, D, K, L), f32),
            pltpu.VMEM((F, D, K, L), f32),
            pltpu.VMEM((D, K // 2, L), f32),
            pltpu.VMEM((D, K // 2, L), f32),
            pltpu.VMEM((D * K, L), f32),
            pltpu.VMEM((PAIRS, D, K, L), f32),
            pltpu.VMEM((PAIRS, D, K, L), f32),
            pltpu.VMEM((2, F, K, L), f32),
            pltpu.VMEM((2, F, K, L), f32),
            pltpu.VMEM((K, L), f32),
            pltpu.VMEM((K, L), f32),
            pltpu.VMEM((F, X, K, L), f32),
            dma((F,)), dma((F,)), dma, dma, dma((PAIRS,)), dma((PAIRS,)),
            dma((2,)), dma((2,)), dma, dma,
            pltpu.VMEM((F, 2, K, L), f32),
            pltpu.VMEM((PAIRS, 2, K, L), f32),
            dma((F,)), dma((PAIRS,)), dma, dma,
        ],
        compiler_params=pltpu.CompilerParams(
            collective_id=0, has_side_effects=True, vmem_limit_bytes=32 * 1024 * 1024
        ),
        name="section_adjoint",
    )(
        *[pltpu.with_memory_space_constraint(v, pltpu.HBM) for v in (adjoint.reshape(F, K * X, L), state.reshape(F, K * X, L), wake.reshape(K * X, L),
        jnp.asarray(high), jnp.asarray(low), jnp.asarray(np.ascontiguousarray(high.T)),
        jnp.asarray(np.ascontiguousarray(low.T)), jac_axial, jac_radial, jac_swirl, wake_coupling)],
    )
    adjoint_in, grad = pl.pallas_call(
        write_out,
        out_shape=(
            jax.ShapeDtypeStruct((F, K * X, L), f32),
            jax.ShapeDtypeStruct((K * X, L), f32),
        ),
        in_specs=[vmem] * 2,
        out_specs=(hbm, hbm),
        scratch_shapes=[dma((2,))],
        compiler_params=pltpu.CompilerParams(vmem_limit_bytes=1024 * 1024),
        name="write_out",
    )(adjoint_in, grad)
    return adjoint_in.reshape(adjoint.shape), grad.reshape(wake.shape)


def solution(mesh):
    return jax.shard_map(
        body,
        mesh=mesh,
        in_specs=(
            P(None, "mode", "ax", "rad"),
            P(None, "mode", "ax", "rad"),
            P("mode", "ax", "rad"),
            P(),
            P(),
            P(),
            P(),
        ),
        out_specs=(P(None, "mode", "ax", "rad"), P("mode", "ax", "rad")),
        check_vma=False,
    )
```

```python
import functools
import math

import jax
import jax.numpy as jnp
import ml_dtypes
import numpy as np
from jax import lax
from jax.experimental import pallas as pl
from jax.experimental.pallas import tpu as pltpu
from jax.sharding import PartitionSpec as P

MESH = pl.DeviceIdType.MESH
F, K, X, L = 5, 32, 4, 128
D = 8
HALF = L // 2
PAIRS = 3
ORDER = (4, 5, 3, 2, 6, 7, 1)


def basis_parts():
    t = np.arange(D * K)[:, None]
    k = np.arange(D * K)[None, :]
    phase = ((k // 2) * t % (D * K)) * (2.0 * math.pi / (D * K))
    table = math.sqrt(2.0 / (D * K)) * np.where(k % 2 == 0, np.cos(phase), np.sin(phase))
    one = 1.0 / math.sqrt(D * K)
    table = np.where(k == 0, one, table)
    table = np.where(k == 1, np.where(t % 2 == 0, one, -one), table)
    high = table.astype(ml_dtypes.bfloat16)
    low = (table - high.astype(np.float64)).astype(ml_dtypes.bfloat16)
    return high, low


def product(high, low, x):
    x_high = x.astype(jnp.bfloat16)
    x_low = (x - x_high.astype(jnp.float32)).astype(jnp.bfloat16)
    dot = functools.partial(jnp.dot, preferred_element_type=jnp.float32)
    return dot(high, x_high) + (dot(high, x_low) + dot(low, x_high))


def kernel(
    adj_hbm, state_hbm, wake_hbm, bh_hbm, bl_hbm, th_hbm, tl_hbm, ja_hbm, jr_hbm, js_hbm, wc_hbm,
    out_ref, grad_ref,
    adj_ref, state_ref, wake_ref, bh_ref, bl_ref, th_ref, tl_ref, ja_ref, jr_ref, js_ref, wc_ref, in_sem,
    send, recv, wsend, wrecv, wfull, back, ret, hsend, hrecv, esend, erecv, acc,
    f_ssem, f_rsem, w_ssem, w_rsem, b_ssem, b_rsem, h_ssem, h_rsem, e_ssem, e_rsem,
):
    me = lax.axis_index("mode")
    ax = lax.axis_index("ax")
    rad = lax.axis_index("rad")
    ax_count = lax.axis_size("ax")
    has_up = ax < ax_count - 1
    has_down = ax > 0
    others = [lax.rem(me + i, D) for i in ORDER]

    barrier = pltpu.get_barrier_semaphore()
    for other in others:
        pl.semaphore_signal(barrier, inc=1, device_id={"mode": other}, device_id_type=MESH)

    @pl.when(has_up)
    def _():
        pl.semaphore_signal(barrier, inc=1, device_id={"ax": ax + 1}, device_id_type=MESH)

    @pl.when(has_down)
    def _():
        pl.semaphore_signal(barrier, inc=1, device_id={"ax": ax - 1}, device_id_type=MESH)

    pl.semaphore_signal(barrier, inc=1, device_id={"rad": 1 - rad}, device_id_type=MESH)

    sources = (adj_hbm, state_hbm, wake_hbm, bh_hbm, bl_hbm, th_hbm, tl_hbm, ja_hbm, jr_hbm, js_hbm, wc_hbm)
    targets = (adj_ref, state_ref, wake_ref, bh_ref, bl_ref, th_ref, tl_ref, ja_ref, jr_ref, js_ref, wc_ref)
    loads = [pltpu.make_async_copy(a, b, in_sem.at[i]) for i, (a, b) in enumerate(zip(sources, targets))]
    for i in (10, 1, 0, 2, 3, 4, 5, 6, 7, 8, 9):
        loads[i].start()

    lane = lax.broadcasted_iota(jnp.int32, (K, L), 1)
    low_half = lane < HALF

    def cells(ref, f, x):
        return ref[f, pl.ds(x, K, stride=X), :]

    def swap(v):
        return pltpu.roll(v, HALF, axis=1)

    def go(src, dst, ssem, rsem, device):
        copy = pltpu.make_async_remote_copy(
            src_ref=src, dst_ref=dst, send_sem=ssem, recv_sem=rsem, device_id=device, device_id_type=MESH
        )
        copy.start()
        return copy

    for i in (10, 1, 0):
        loads[i].wait()
    q = K // 2
    for f in range(F):
        for x in range(X):
            a = cells(adj_ref, f, x)
            c = wc_ref[f, 0] * cells(state_ref, 0, x)
            for e in range(1, F):
                c = c + wc_ref[f, e] * cells(state_ref, e, x)
            send[f, 2 * x] = jnp.where(low_half, a, swap(c))
            send[f, 2 * x + 1] = jnp.where(low_half, swap(a), c)
        if f == 0:
            loads[2].wait()
            for x in range(X):
                w = wake_ref[pl.ds(x, K, stride=X), :]
                w_swap = swap(w)
                m = low_half[:q]
                wsend[2 * x] = jnp.where(m, w[:q], w_swap[q:])
                wsend[2 * x + 1] = jnp.where(m, w_swap[:q], w[q:])
            pl.semaphore_wait(barrier, D + has_up.astype(jnp.int32) + has_down.astype(jnp.int32))
        for other in others:
            go(send.at[f, other], recv.at[f, me], f_ssem.at[f], f_rsem.at[f], {"mode": other})
        if f == 0:
            for other in others:
                go(wsend.at[other], wrecv.at[me], w_ssem, w_rsem, {"mode": other})

    edge = jnp.zeros((K, L), jnp.float32)
    for f in range(F):
        hsend[0, f] = cells(adj_ref, f, 0)
        hsend[1, f] = cells(adj_ref, f, X - 1)
        for x in range(X):
            s = f * X + x
            v = cells(adj_ref, f, x)
            v = jnp.where(rad == 0, pltpu.roll(v, s + 1, axis=1), pltpu.roll(v, s, axis=1) if s else v)
            edge = jnp.where(lane == s, v, edge)
    esend[...] = edge

    @pl.when(has_down)
    def _():
        go(hsend.at[0], hrecv.at[1], h_ssem.at[0], h_rsem.at[1], {"ax": ax - 1})

    @pl.when(has_up)
    def _():
        go(hsend.at[1], hrecv.at[0], h_ssem.at[1], h_rsem.at[0], {"ax": ax + 1})

    go(esend, erecv, e_ssem, e_rsem, {"rad": 1 - rad})

    wrecv[me] = wsend[me]
    for f in range(F):
        recv[f, me] = send[f, me]

    def whole(ref, sem):
        return pltpu.make_async_remote_copy(
            src_ref=ref, dst_ref=ref, send_sem=sem, recv_sem=sem, device_id={"rad": 1 - rad}, device_id_type=MESH
        )

    seven = pl.ds(0, D - 1)

    whole(wrecv.at[seven], w_rsem).wait_recv()
    for d in range(D):
        w = wrecv[d]
        w_swap = swap(w)
        m = low_half[:q]
        wfull[pl.ds(d * K, q), :] = jnp.where(m, w, w_swap)
        wfull[pl.ds(d * K + q, q), :] = jnp.where(m, w_swap, w)

    for i in (3, 4, 5, 6, 7, 8, 9):
        loads[i].wait()
    low_all = lax.broadcasted_iota(jnp.int32, (D * K, L), 1) < HALF
    total = None
    first = None
    for f in range(F):
        whole(recv.at[f, seven], f_rsem.at[f]).wait_recv()
        angle = product(bh_ref[...], bl_ref[...], recv[f].reshape(D * K, L))
        angle_swap = swap(angle)
        term = angle * angle_swap
        total = term if total is None else total + term
        wake_all = wfull[...]
        if f % 2 == 0 and f < F - 1:
            first = wake_all * angle
            continue
        p = f // 2
        if f < F - 1:
            both = jnp.where(low_all, first, wake_all * angle_swap)
        else:
            both = wake_all * angle
        if f == F - 1:
            n = D * K // 2
            for part in range(2):
                rows = pl.ds(part * n, n)
                result = product(th_ref[rows, :], tl_ref[rows, :], both)
                result = jnp.where(low_all[:n], result, -total[part * n : (part + 1) * n])
                back[p, pl.ds(part * D // 2, D // 2)] = result.reshape(D // 2, K, L)
                for d in range(part * D // 2, (part + 1) * D // 2):

                    @pl.when(me != d)
                    def _():
                        go(back.at[p, d], ret.at[p, me], b_ssem.at[p], b_rsem.at[p], {"mode": d})

            ret[p, me] = back[p, me]
            break
        result = product(th_ref[...], tl_ref[...], both)
        back[p] = result.reshape(D, K, L)
        for other in others:
            go(back.at[p, other], ret.at[p, me], b_ssem.at[p], b_rsem.at[p], {"mode": other})
        ret[p, me] = back[p, me]

    @pl.when(has_down)
    def _():
        whole(hrecv.at[0], h_rsem.at[0]).wait_recv()
        whole(hsend.at[0], h_ssem.at[0]).wait_send()

    @pl.when(has_up)
    def _():
        whole(hrecv.at[1], h_rsem.at[1]).wait_recv()
        whole(hsend.at[1], h_ssem.at[1]).wait_send()

    whole(erecv, e_rsem).wait_recv()
    whole(esend, e_ssem).wait_send()
    whole(wsend.at[seven], w_ssem).wait_send()
    for f in range(F):
        whole(send.at[f, seven], f_ssem.at[f]).wait_send()
    row = lax.broadcasted_iota(jnp.int32, (K, L), 0)
    even = lax.rem(row, 2) == 0
    order = lax.div(me * K + row, 2).astype(jnp.float32) / jnp.float32(D * K // 2)
    radius = 0.5 + ((rad * L + lane).astype(jnp.float32) + 0.5) / jnp.float32(4.0 * L)
    rate = (0.25 / radius) * order
    rate = jnp.where(even, rate, -rate)
    nearby = erecv[...]
    nearby_up = jnp.where(rad == 0, nearby, 0.0)
    nearby_down = jnp.where(rad == 1, nearby, 0.0)
    for x in range(X):
        fields, axial, radial, turned = [], [], [], []
        for e in range(F):
            a = cells(adj_ref, e, x)
            fields.append(a)
            if x == X - 1:
                above = jnp.where(has_up, hrecv[1, e], 0.0)
            else:
                above = cells(adj_ref, e, x + 1)
            if x == 0:
                below = jnp.where(has_down, hrecv[0, e], 0.0)
            else:
                below = cells(adj_ref, e, x - 1)
            axial.append(0.5 * (above - below))
            s = e * X + x
            up = jnp.where(lane == L - 1, pltpu.roll(nearby_up, L - 1 - s, axis=1), pltpu.roll(a, L - 1, axis=1))
            edge_down = pltpu.roll(nearby_down, L - s, axis=1) if s else nearby_down
            down = jnp.where(lane == 0, edge_down, pltpu.roll(a, 1, axis=1))
            radial.append(0.5 * (up - down))
            turned.append(rate * jnp.where(even, pltpu.roll(a, K - 1, axis=0), pltpu.roll(a, 1, axis=0)))
        for f in range(F):
            v = fields[f]
            for e in range(F):
                v = v + ja_ref[e, f] * axial[e] + jr_ref[e, f] * radial[e] + js_ref[e, f] * turned[e]
            acc[f, x] = v

    def pair(p, x):
        one, two = ret[p, 2 * x], ret[p, 2 * x + 1]
        return jnp.where(low_half, one, swap(two)), jnp.where(low_half, swap(one), two)

    for p in range(PAIRS - 1):
        whole(ret.at[p, seven], b_rsem.at[p]).wait_recv()
        whole(back.at[p, seven], b_ssem.at[p]).wait_send()
    for x in range(X):
        returned = [v for p in range(PAIRS - 1) for v in pair(p, x)]
        for f in range(F):
            v = acc[f, x]
            for e in range(F - 1):
                v = v - wc_ref[e, f] * returned[e]
            acc[f, x] = v
    p = PAIRS - 1
    whole(back.at[p, seven], b_ssem.at[p]).wait_send()
    whole(ret.at[p, seven], b_rsem.at[p]).wait_recv()
    for x in range(X):
        last, grad = pair(p, x)
        grad_ref[pl.ds(x, K, stride=X), :] = grad
        for f in range(F):
            out_ref[f, pl.ds(x, K, stride=X), :] = acc[f, x] - wc_ref[F - 1, f] * last


def write_out(field_ref, grad_ref, field_out, grad_out, sem):
    copies = [
        pltpu.make_async_copy(field_ref, field_out, sem.at[0]),
        pltpu.make_async_copy(grad_ref, grad_out, sem.at[1]),
    ]
    for copy in copies:
        copy.start()
    for copy in copies:
        copy.wait()


def body(adjoint, state, wake, jac_axial, jac_radial, jac_swirl, wake_coupling):
    high, low = basis_parts()
    vmem = pl.BlockSpec(memory_space=pltpu.VMEM)
    hbm = pl.BlockSpec(memory_space=pltpu.HBM)
    dma = pltpu.SemaphoreType.DMA
    f32 = jnp.float32
    adjoint_in, grad = pl.pallas_call(
        kernel,
        out_shape=(
            jax.ShapeDtypeStruct((F, K * X, L), f32),
            jax.ShapeDtypeStruct((K * X, L), f32),
        ),
        in_specs=[hbm] * 11,
        out_specs=(vmem, vmem),
        scratch_shapes=[
            pltpu.VMEM((F, K * X, L), f32),
            pltpu.VMEM((F, K * X, L), f32),
            pltpu.VMEM((K * X, L), f32),
            *[pltpu.VMEM((D * K, D * K), jnp.bfloat16)] * 4,
            *[pltpu.SMEM((F, F), f32)] * 4,
            dma((11,)),
            pltpu.VMEM((F, D, K, L), f32),
            pltpu.VMEM((F, D, K, L), f32),
            pltpu.VMEM((D, K // 2, L), f32),
            pltpu.VMEM((D, K // 2, L), f32),
            pltpu.VMEM((D * K, L), f32),
            pltpu.VMEM((PAIRS, D, K, L), f32),
            pltpu.VMEM((PAIRS, D, K, L), f32),
            pltpu.VMEM((2, F, K, L), f32),
            pltpu.VMEM((2, F, K, L), f32),
            pltpu.VMEM((K, L), f32),
            pltpu.VMEM((K, L), f32),
            pltpu.VMEM((F, X, K, L), f32),
            dma((F,)), dma((F,)), dma, dma, dma((PAIRS,)), dma((PAIRS,)),
            dma((2,)), dma((2,)), dma, dma,
        ],
        compiler_params=pltpu.CompilerParams(
            collective_id=0, has_side_effects=True, vmem_limit_bytes=32 * 1024 * 1024
        ),
        name="section_adjoint",
    )(
        *[pltpu.with_memory_space_constraint(v, pltpu.HBM) for v in (adjoint.reshape(F, K * X, L), state.reshape(F, K * X, L), wake.reshape(K * X, L),
        jnp.asarray(high), jnp.asarray(low), jnp.asarray(np.ascontiguousarray(high.T)),
        jnp.asarray(np.ascontiguousarray(low.T)), jac_axial, jac_radial, jac_swirl, wake_coupling)],
    )
    adjoint_in, grad = pl.pallas_call(
        write_out,
        out_shape=(
            jax.ShapeDtypeStruct((F, K * X, L), f32),
            jax.ShapeDtypeStruct((K * X, L), f32),
        ),
        in_specs=[vmem] * 2,
        out_specs=(hbm, hbm),
        scratch_shapes=[dma((2,))],
        compiler_params=pltpu.CompilerParams(vmem_limit_bytes=1024 * 1024),
        name="write_out",
    )(adjoint_in, grad)
    return adjoint_in.reshape(adjoint.shape), grad.reshape(wake.shape)


def solution(mesh):
    return jax.shard_map(
        body,
        mesh=mesh,
        in_specs=(
            P(None, "mode", "ax", "rad"),
            P(None, "mode", "ax", "rad"),
            P("mode", "ax", "rad"),
            P(),
            P(),
            P(),
            P(),
        ),
        out_specs=(P(None, "mode", "ax", "rad"), P("mode", "ax", "rad")),
        check_vma=False,
    )
```
